512 devices in a mesh: row: 64 (over z, y_lo, x), col: 8 (over y_hi, core).
Axes of the slice: x: 4, y: 8 (y_hi: 4, y_lo: 2; y = y_hi * 2 + y_lo), z: 8, core: 2. Of those that a mesh axis runs over, the one named last changes fastest.
Arguments:
- trailing: bfloat16 [32768, 4096], P('row', 'col'), may hold values from -6 to 6
- u_factor: bfloat16 [64, 8, 512, 256], P('row', 'col'), may hold values from -0.07861328 to 0.07861328
- w_factor: bfloat16 [64, 8, 512, 256], P('row', 'col'), may hold values from -4.1875 to 4.1875
- diag_inverse: bfloat16 [8, 512, 512], P('col'), as said below
- ranks: int32 [64, 8], P('row', 'col'), may hold values from 32 to 256, as said below
- col_rows: int32 [8], replicated, may hold values from 0 to 63, as said below
Outputs:
- updated: float32 [32768, 4096], P('row', 'col')
The draws below stay inside these ranges and needn't reach their ends.
Inputs may be any that keep to these rules, and one draw needn't show every extreme that they name: `ranks`: each tile's rank; some tile has rank 256 and some has rank 256 // 8. `col_rows`: distinct tile rows. `diag_inverse`: lower triangular, diagonal between 0.5 and 2.
All inputs are finite; a program needn't handle non-finite values.
Results may differ from the reference program's by a relative error of at most 0.0047.
Values may be sent and summed in bfloat16 or wider, within the bound.
A program may use at most 64 MiB of HBM per device.

```python
import jax
import jax.numpy as jnp
from jax import lax

TILE = 512
RMAX = 256
PANELS = 8
ROWS = 64
COLS = 8


def draw_diag_inverse(key, part):
    first, second = jax.random.split(jax.random.fold_in(key, 11))
    lower = jax.random.normal(first, (PANELS, TILE, TILE), jnp.float32) / TILE ** 0.5
    lower = jnp.tril(lower, -1)
    diag_values = jnp.exp(jax.random.uniform(second, (PANELS, TILE), jnp.float32, jnp.log(0.5), jnp.log(2.0)))
    eye = jnp.eye(TILE, dtype=jnp.float32)
    return (lower + eye[None, :, :] * diag_values[:, :, None]).astype(jnp.bfloat16)


def draw_ranks(key, part):
    values = jax.random.randint(jax.random.fold_in(key, 23), (ROWS, PANELS), RMAX // 8, RMAX + 1)
    values = values.at[0, 0].set(RMAX)
    values = values.at[ROWS - 1, PANELS - 1].set(RMAX // 8)
    return values.astype(jnp.int32)


def draw_col_rows(key, part):
    inner = jax.random.permutation(jax.random.fold_in(key, 37), max(ROWS - 2, 1))[:COLS - 2].astype(jnp.int32) + 1
    ends = jnp.array([0, ROWS - 1], dtype=jnp.int32)
    chosen = jnp.concatenate([ends, inner])
    order = jax.random.permutation(jax.random.fold_in(key, 41), COLS)
    return chosen[order].astype(jnp.int32)


def steps_of(rng, extent, cuts, least, largest):
    factor_of, own = 1.0, jax.random.fold_in(rng, 6)
    for axis_at, parts in cuts:
        heights = jnp.exp(jax.random.uniform(jax.random.fold_in(own, axis_at), (parts,), jnp.float32, least / len(cuts), largest / len(cuts)))
        factor_of = factor_of * jnp.repeat(heights, extent[axis_at] // parts).reshape([-1 if axis == axis_at else 1 for axis in range(len(extent))])
    return factor_of


def noise(key, extent, scale, most, pieces=(), held_as=jnp.bfloat16):
    values = jax.random.normal(key, extent, jnp.float32) * scale
    if len(pieces) > 0:
        values = steps_of(key, extent, pieces, -0.22, 0.18) * values
    return jnp.clip(values, min=-most, max=most).astype(held_as)


def setup_inputs(seed: int = 0) -> dict:
    key_of = jax.random.split(jax.random.key(seed), 7)
    return {
        "trailing": noise(key_of[0], (ROWS * TILE, COLS * TILE), 1.0, 6.0, ((0, 64), (1, 8))),
        "u_factor": noise(key_of[1], (ROWS, PANELS, TILE, RMAX), ((RMAX * TILE ** 0.5) ** -0.5), 0.07861328, ((0, 64), (1, 8))),
        "w_factor": noise(key_of[2], (ROWS, PANELS, TILE, RMAX), 0.7, 4.1875, ((0, 64), (1, 8))),
        "diag_inverse": draw_diag_inverse(jax.random.fold_in(key_of[6], 71), 0),
        "ranks": draw_ranks(jax.random.fold_in(key_of[6], 71), 0),
        "col_rows": draw_col_rows(jax.random.fold_in(key_of[6], 71), 0),
    }


def reference(trailing, u_factor, w_factor, diag_inverse, ranks, col_rows):
    product = jnp.einsum('ktu,ikur->iktr', diag_inverse.astype(jnp.float32), w_factor.astype(jnp.float32))
    keep = jnp.arange(RMAX, dtype=jnp.int32)[None, None, :] < ranks[:, :, None]
    solved = jnp.where(keep[:, :, None, :], product.astype(jnp.bfloat16), jnp.zeros((), jnp.bfloat16))
    col_u = u_factor[col_rows].astype(jnp.float32)
    col_v = solved[col_rows].astype(jnp.float32)
    tiles = trailing.reshape(ROWS, TILE, COLS, TILE)

    def one_row(items):
        u_row, v_row, c_row = items
        core = jnp.einsum('ktr,ckts->ckrs', v_row.astype(jnp.float32), col_v).astype(jnp.bfloat16)
        mixed = jnp.einsum('ktr,ckrs->ckts', u_row.astype(jnp.float32), core.astype(jnp.float32)).astype(jnp.bfloat16)
        change = jnp.einsum('ckts,ckus->tcu', mixed.astype(jnp.float32), col_u)
        return c_row.astype(jnp.float32) - change

    result = lax.map(one_row, (u_factor, solved, tiles))
    return result.reshape(ROWS * TILE, COLS * TILE)
```

```python
import jax
import jax.numpy as jnp
from jax import lax
from jax.sharding import PartitionSpec as P


def panel_update(left_rows, right_rows, left_cols, right_cols):
    core = jnp.einsum(
        "ktr,kts->krs", right_rows, right_cols, preferred_element_type=jnp.float32
    ).astype(jnp.bfloat16)
    mixed = jnp.einsum("ktr,krs->kts", left_rows, core, preferred_element_type=jnp.float32).astype(
        jnp.bfloat16
    )
    return jnp.einsum("kts,kus->tu", mixed, left_cols, preferred_element_type=jnp.float32)


def local(trailing, u_factor, w_factor, diag_inverse, ranks, col_rows):
    tile, rank_max = w_factor.shape[2:]
    rows = lax.axis_size("row")
    product = jnp.einsum(
        "ktu,kur->ktr", diag_inverse, w_factor[0], preferred_element_type=jnp.float32
    )
    keep = jnp.arange(rank_max, dtype=jnp.int32)[None, :] < ranks[0][:, None]
    solved = jnp.where(keep[:, None, :], product.astype(jnp.bfloat16), jnp.zeros((), jnp.bfloat16))
    paired = jnp.concatenate([u_factor[0], solved], axis=1)
    pieces = paired.reshape(rows, 2 * tile // rows, rank_max)
    spread = lax.all_to_all(pieces, "row", 0, 0, tiled=True)
    chosen = jnp.take(spread, col_rows, axis=0)
    mine = lax.all_to_all(chosen, "col", 0, 0, tiled=True)
    column = lax.all_gather(mine, "row", axis=1, tiled=True)
    gathered = lax.all_gather(paired, "col", axis=0, tiled=True)
    base = trailing.astype(jnp.float32)
    result = base - panel_update(
        gathered[:, :tile], gathered[:, tile:], column[:, :tile], column[:, tile:]
    )
    return result


def solution(mesh):
    placed = (
        P("row", "col"),
        P("row", "col", None, None),
        P("row", "col", None, None),
        P("col", None, None),
        P("row", "col"),
        P(),
    )
    return jax.shard_map(
        local, mesh=mesh, in_specs=placed, out_specs=P("row", "col"), check_vma=False
    )
```

```python
import jax
import jax.numpy as jnp
from jax import lax
from jax.experimental import pallas as pl
from jax.experimental.pallas import tpu as pltpu
from jax.sharding import PartitionSpec as P

MESH = pl.DeviceIdType.MESH
ROWS, COLS = 64, 8
NX, NY, NZ, NH = 4, 2, 8, 4
TILE, RANK = 512, 256
BOTH = 2 * TILE
PIECE = BOTH // ROWS
STEP = NY * PIECE
SLAB = NX * STEP
FIRST = 3


def aligned(value, factor):
    return pl.multiple_of(value * factor, factor)


def kernel(
    pairs, ranks, trailing, u_ref, w_ref, inverse, out,
    mine, theirs, landed, picked,
    spread_sem, place_sem, ring_sems, x_sems, z_sems, wide_x_sems, wide_z_sems,
):
    row, col = lax.axis_index("row"), lax.axis_index("col")
    z, y, x = row // (NX * NY), (row // NX) % NY, row % NX
    h, core = col // 2, col % 2

    def at(new_z, new_y, new_x):
        return (new_z * NY + new_y) * NX + new_x

    def piece_of(other):
        return (other // (NX * NY)) * (NX * NY) + (other % NX) * NY + (other // NX) % NY

    partner = at(z, 1 - y, x)

    barrier = pltpu.get_barrier_semaphore()

    @pl.loop(1, ROWS)
    def _(d):
        pl.semaphore_signal(barrier, inc=1, device_id=((row + d) % ROWS, col), device_id_type=MESH)

    @pl.loop(1, COLS)
    def _(d):
        other = (col + d) % COLS
        pl.semaphore_signal(barrier, inc=1, device_id=(row, other), device_id_type=MESH)
        pl.semaphore_signal(barrier, inc=1, device_id=(partner, other), device_id_type=MESH)

    product = jnp.dot(inverse[0], w_ref[0, 0], preferred_element_type=jnp.float32)
    lane = lax.broadcasted_iota(jnp.int32, (TILE, RANK), 1)
    solved = jnp.where(lane < ranks[0, 0], product, 0.0).astype(jnp.bfloat16)
    mine[col, TILE:, :] = solved
    mine[col, :TILE, :] = u_ref[0, 0]

    pl.semaphore_wait(barrier, ROWS - 1 + 2 * (COLS - 1))

    sent = []

    def send(source, target, send_sem, recv_sem, to_row, to_col):
        copy = pltpu.make_async_remote_copy(
            src_ref=source, dst_ref=target, send_sem=send_sem, recv_sem=recv_sem,
            device_id=(to_row, to_col), device_id_type=MESH,
        )
        copy.start()
        sent.append(copy)

    def arrived(target, sem):
        pltpu.make_async_copy(target, target, sem).wait()

    own_piece = aligned(piece_of(row), PIECE)
    landed[row] = mine[col, pl.ds(own_piece, PIECE), :]

    @pl.loop(1, ROWS)
    def _(d):
        other = (row + d) % ROWS
        pltpu.make_async_remote_copy(
            src_ref=mine.at[col, pl.ds(aligned(piece_of(other), PIECE), PIECE), :],
            dst_ref=landed.at[row],
            send_sem=spread_sem.at[0], recv_sem=spread_sem.at[1],
            device_id=(other, col), device_id_type=MESH,
        ).start()

    right, left = ((h + 1) % NH) * 2 + core, ((h + NH - 1) % NH) * 2 + core
    across, twin = ((h + 2) % NH) * 2 + core, col + 1 - 2 * core
    halves = (pl.ds(0, TILE), pl.ds(TILE, TILE))
    count = [0]

    def pass_on(panel, half, to, slot):
        block = mine.at[panel, halves[half], :]
        send(block, block, ring_sems.at[0, count[0]], ring_sems.at[1, slot], row, to)
        count[0] += 1

    def ring_arrived(panel, half, slot):
        arrived(mine.at[panel, halves[half], :], ring_sems.at[1, slot])

    pass_on(col, 0, right, 0)
    pass_on(col, 1, left, 3)
    pass_on(col, 1, right, 1)
    pass_on(col, 0, left, 2)
    pass_on(col, 0, twin, 6)
    pass_on(col, 1, twin, 7)

    arrived(landed.at[pl.ds(0, ROWS - 1)], spread_sem.at[1])
    chosen = picked
    spot = (col, pl.ds(own_piece, PIECE), slice(None))
    for c in range(COLS):
        chosen[c] = landed[pairs[c]]

    @pl.loop(1, COLS)
    def _(d):
        other = (col + d) % COLS
        for to_row in (row, partner):
            pltpu.make_async_remote_copy(
                src_ref=chosen.at[other], dst_ref=theirs.at[spot],
                send_sem=place_sem.at[0], recv_sem=place_sem.at[1],
                device_id=(to_row, other), device_id_type=MESH,
            ).start()

    pltpu.make_async_remote_copy(
        src_ref=chosen.at[col], dst_ref=theirs.at[spot],
        send_sem=place_sem.at[0], recv_sem=place_sem.at[1],
        device_id=(partner, col), device_id_type=MESH,
    ).start()
    theirs[spot] = chosen[col]
    arrived(landed.at[pl.ds(0, 2 * COLS - 1)], place_sem.at[1])

    few, many = pl.ds(0, FIRST), pl.ds(FIRST, COLS - FIRST)
    x_side = (at(z, y, (x + 1) % NX), at(z, y, (x + NX - 1) % NX))
    z_side = (at((z + 1) % NZ, y, x), at((z + NZ - 1) % NZ, y, x))

    def x_from(way, hops):
        return (x + NX - hops) % NX if way == 0 else (x + hops) % NX

    def z_from(way, hops):
        return (z + NZ - hops) % NZ if way == 0 else (z + hops) % NZ

    def small(panels, from_z, from_x, half=None):
        start = from_z * SLAB + from_x * STEP
        if half is None:
            return theirs.at[panels, pl.ds(pl.multiple_of(start, STEP), STEP), :]
        start = pl.multiple_of(start + half * PIECE, PIECE)
        return theirs.at[panels, pl.ds(start, PIECE), :]

    def large(panel, from_z, half=None):
        if half is None:
            return theirs.at[panel, pl.ds(aligned(from_z, SLAB), SLAB), :]
        return theirs.at[panel, pl.ds(aligned(from_z * 2 + half, SLAB // 2), SLAB // 2), :]

    def send_x(block, way, slot):
        send(block, block, x_sems.at[0, way, slot], x_sems.at[1, way, slot], x_side[way], col)

    def send_z(block, way, panel, slot):
        sems = z_sems
        send(block, block, sems.at[0, way, panel, slot], sems.at[1, way, panel, slot], z_side[way], col)

    def send_wide_z(block, way, slot):
        sems = wide_z_sems
        send(block, block, sems.at[0, way, slot], sems.at[1, way, slot], z_side[way], col)

    def send_wide_x(block, way, slot):
        sems = wide_x_sems
        send(block, block, sems.at[0, way, slot], sems.at[1, way, slot], x_side[way], col)

    ways = (0, 1)
    order = [(0, 0)] + [(w, s) for s in (1, 2, 3) for w in ways] + [(0, 4)]

    def place_z(entry):
        return z_from(*entry)

    for w in ways:
        send_x(small(few, z, x), w, 0)
    for w in ways:
        send_wide_z(small(many, z, x), w, 0)
    for w in ways:
        send_wide_x(small(many, z, x), w, 0)

    def wide_step(step):
        for w in ways:
            if step < 4:
                arrived(small(many, z_from(w, step), x), wide_z_sems.at[1, w, step - 1])
            else:
                arrived(small(many, z_from(w, step), x, w), wide_z_sems.at[1, w, step - 1])
            if step < 3:
                send_wide_z(small(many, z_from(w, step), x), w, step)
            elif step == 3:
                send_wide_z(small(many, z_from(w, step), x, w), w, step)
        if step < 4:
            for w in ways:
                slot = order.index((w, step))
                for v in ways:
                    send_wide_x(small(many, z_from(w, step), x), v, slot)
        else:
            for v in ways:
                send_wide_x(small(many, z_from(0, 4), x), v, 7)

    def second_hop(slots):
        for slot in slots:
            from_z = place_z(order[slot])
            for v in ways:
                arrived(small(many, from_z, x_from(v, 1)), wide_x_sems.at[1, v, slot])
            v = slot % 2
            send_wide_x(small(many, from_z, x_from(v, 1)), v, 8 + slot // 2)

    for w in ways:
        arrived(small(few, z, x_from(w, 1)), x_sems.at[1, w, 0])
        send_x(small(few, z, x_from(w, 1), w), w, 1)
    wide_step(1)
    for w in ways:
        arrived(small(few, z, x_from(w, 2), w), x_sems.at[1, w, 1])
    for k in range(FIRST):
        for w in ways:
            send_z(large(k, z), w, k, 0)
    wide_step(2)
    second_hop([0])
    ring_arrived(left, 0, 0)
    pass_on(left, 0, right, 4)
    ring_arrived(right, 1, 3)
    pass_on(right, 1, left, 5)
    wide_step(3)
    for k in range(FIRST):
        for w in ways:
            arrived(large(k, z_from(w, 1)), z_sems.at[1, w, k, 0])
            send_z(large(k, z_from(w, 1)), w, k, 1)
    second_hop([1, 2])
    wide_step(4)
    for k in range(FIRST):
        for w in ways:
            arrived(large(k, z_from(w, 2)), z_sems.at[1, w, k, 1])
            send_z(large(k, z_from(w, 2)), w, k, 2)
    second_hop([3, 4])
    pass_on(left, 0, twin, 8)
    pass_on(right, 1, twin, 11)
    ring_arrived(left, 1, 1)
    pass_on(left, 1, twin, 9)
    ring_arrived(right, 0, 2)
    pass_on(right, 0, twin, 10)
    for k in range(FIRST):
        for w in ways:
            arrived(large(k, z_from(w, 3)), z_sems.at[1, w, k, 2])
            send_z(large(k, z_from(w, 3), w), w, k, 3)
    second_hop([5, 6])
    second_hop([7])
    ring_arrived(across, 0, 4)
    pass_on(across, 0, twin, 12)
    ring_arrived(across, 1, 5)
    pass_on(across, 1, twin, 13)
    for k in range(FIRST):
        for w in ways:
            arrived(large(k, z_from(w, 4), w), z_sems.at[1, w, k, 3])
    for slot in range(8):
        v = slot % 2
        from_z = place_z(order[slot])
        arrived(small(many, from_z, x_from(v, 2)), wide_x_sems.at[1, v, 8 + slot // 2])
    flip = 1 - 2 * core
    for panel, base in ((twin, 6), (left + flip, 8), (right + flip, 10), (across + flip, 12)):
        ring_arrived(panel, 0, base)
        ring_arrived(panel, 1, base + 1)

    out[...] = trailing[...].astype(jnp.float32)

    @pl.loop(0, COLS)
    def _(k):
        middle = lax.dot_general(
            mine[k, TILE:, :], theirs[k, TILE:, :], (((0,), (0,)), ((), ())),
            preferred_element_type=jnp.float32,
        ).astype(jnp.bfloat16)
        mixed = jnp.dot(
            mine[k, :TILE, :], middle, preferred_element_type=jnp.float32
        ).astype(jnp.bfloat16)
        out[...] -= lax.dot_general(
            mixed, theirs[k, :TILE, :], (((1,), (1,)), ((), ())),
            preferred_element_type=jnp.float32,
        )

    for copy in sent:
        copy.wait_send()
    arrived(landed.at[pl.ds(0, ROWS - 1)], spread_sem.at[0])
    arrived(landed.at[pl.ds(0, 2 * COLS - 1)], place_sem.at[0])


def local(trailing, u_factor, w_factor, diag_inverse, ranks, col_rows):
    vmem, smem = pl.BlockSpec(memory_space=pltpu.VMEM), pl.BlockSpec(memory_space=pltpu.SMEM)
    sems = pltpu.SemaphoreType.DMA
    return pl.pallas_call(
        kernel,
        out_shape=jax.ShapeDtypeStruct((TILE, TILE), jnp.float32),
        in_specs=[smem, smem, vmem, vmem, vmem, vmem],
        out_specs=vmem,
        scratch_shapes=[
            pltpu.VMEM((COLS, BOTH, RANK), jnp.bfloat16),
            pltpu.VMEM((COLS, BOTH, RANK), jnp.bfloat16),
            pltpu.VMEM((ROWS, PIECE, RANK), jnp.bfloat16),
            pltpu.VMEM((COLS, PIECE, RANK), jnp.bfloat16),
            sems((2,)),
            sems((2,)),
            sems((2, 14)),
            sems((2, 2, 2)),
            sems((2, 2, FIRST, 4)),
            sems((2, 2, 12)),
            sems((2, 2, 4)),
        ],
        compiler_params=pltpu.CompilerParams(
            collective_id=0, has_side_effects=True, vmem_limit_bytes=40 * 2**20
        ),
    )(col_rows, ranks, trailing, u_factor, w_factor, diag_inverse)


def solution(mesh):
    placed = (
        P("row", "col"),
        P("row", "col", None, None),
        P("row", "col", None, None),
        P("col", None, None),
        P("row", "col"),
        P(),
    )
    return jax.shard_map(
        local, mesh=mesh, in_specs=placed, out_specs=P("row", "col"), check_vma=False
    )
```

```python
import jax
import jax.numpy as jnp
from jax import lax
from jax.experimental import pallas as pl
from jax.experimental.pallas import tpu as pltpu
from jax.sharding import PartitionSpec as P

MESH = pl.DeviceIdType.MESH
ROWS, COLS = 64, 8
NX, NY, NZ, NH = 4, 2, 8, 4
TILE, RANK = 512, 256
LANES = RANK // NY
STEP = TILE // (NX * NZ)
SLAB = NX * STEP
WAYS = (0, 1)
GROUPS = ((0, 3), (3, 2), (5, 3))
PLAN = (
    0, 1, 3, 5, 5, 1, 1, 3, 3, 0, 2, 4, 1, 1, 2, 2, 3, 3, 5, 5, 4, 0, 0, 4, 0, 0, 0, 0, 2, 1, 1, 2,
    3, 3, 4, 0, 0, 4, 0, 0, 2, 0, 0, 2, 1, 3, 5, 5, 4, 0, 0, 4, 0, 0, 0, 0, 2, 4, 5, 0, 2, 4,
)
ORDER = [(0, 0)] + [(w, s) for s in (1, 2, 3) for w in WAYS] + [(0, 4)]


def kernel(
    pairs, ranks, trailing, u_ref, w_ref, inverse_ref, out,
    mine, theirs, landed, picked, base, w, inverse,
    load_sems, own_sems, spread_sems, place_sems, ring_sems,
    x_sems, z_sems, wide_x_sems, wide_z_sems,
):
    row, col = lax.axis_index("row"), lax.axis_index("col")
    z, y, x = row // (NX * NY), (row // NX) % NY, row % NX
    h, core = col // 2, col % 2

    def at(new_z, new_y, new_x):
        return (new_z * NY + new_y) * NX + new_x

    partner = at(z, 1 - y, x)

    loads = [
        pltpu.make_async_copy(source, target, load_sems.at[i])
        for i, (source, target) in enumerate((
            (inverse_ref.at[0], inverse),
            (w_ref.at[0, 0], w),
            (u_ref.at[0, 0], mine.at[col, 1]),
            (trailing, base),
        ))
    ]
    for load in loads:
        load.start()

    barrier = pltpu.get_barrier_semaphore()

    @pl.loop(1, ROWS)
    def _(d):
        pl.semaphore_signal(barrier, inc=1, device_id=((row + d) % ROWS, col), device_id_type=MESH)

    @pl.loop(1, COLS)
    def _(d):
        other = (col + d) % COLS
        pl.semaphore_signal(barrier, inc=1, device_id=(row, other), device_id_type=MESH)
        pl.semaphore_signal(barrier, inc=1, device_id=(partner, other), device_id_type=MESH)

    loads[0].wait()
    loads[1].wait()
    product = jnp.dot(inverse[...], w[...], preferred_element_type=jnp.float32)
    lane = lax.broadcasted_iota(jnp.int32, (TILE, RANK), 1)
    mine[col, 0] = jnp.where(lane < ranks[0, 0], product, 0.0).astype(jnp.bfloat16)
    loads[2].wait()

    pl.semaphore_wait(barrier, ROWS - 1 + 2 * (COLS - 1))

    sent = []

    def send(source, target, send_sem, recv_sem, to_row, to_col):
        copy = pltpu.make_async_remote_copy(
            src_ref=source, dst_ref=target, send_sem=send_sem, recv_sem=recv_sem,
            device_id=(to_row, to_col), device_id_type=MESH,
        )
        copy.start()
        sent.append(copy)

    def arrived(target, sem):
        pltpu.make_async_copy(target, target, sem).wait()

    def piece(other):
        place = (other // (NX * NY)) * NX + other % NX
        first = pl.multiple_of((other // NX) % NY * LANES, LANES)
        return mine.at[
            col, :, pl.ds(pl.multiple_of(place * STEP, STEP), STEP), pl.ds(first, LANES)
        ]

    own = pltpu.make_async_copy(piece(row), landed.at[row], own_sems.at[0])
    own.start()

    @pl.loop(1, ROWS)
    def _(d):
        other = (row + d) % ROWS
        pltpu.make_async_remote_copy(
            src_ref=piece(other), dst_ref=landed.at[row],
            send_sem=spread_sems.at[0], recv_sem=spread_sems.at[1],
            device_id=(other, col), device_id_type=MESH,
        ).start()

    right, left = ((h + 1) % NH) * 2 + core, ((h + NH - 1) % NH) * 2 + core
    across, twin = ((h + 2) % NH) * 2 + core, col + 1 - 2 * core
    count = [0]

    def pass_on(panel, part, to, slot):
        ref = mine.at[panel, part]
        send(ref, ref, ring_sems.at[0, count[0]], ring_sems.at[1, slot], row, to)
        count[0] += 1

    def ring_arrived(panel, part, slot):
        arrived(mine.at[panel, part], ring_sems.at[1, slot])

    pass_on(col, 0, right, 0)
    pass_on(col, 1, left, 3)

    own.wait()
    arrived(landed.at[pl.ds(0, ROWS - 1)], spread_sems.at[1])
    spot = theirs.at[
        :, col, pl.ds(pl.multiple_of((z * NX + x) * STEP, STEP), STEP),
        pl.ds(pl.multiple_of(y * LANES, LANES), LANES),
    ]
    for c in range(COLS):
        picked[c] = landed[pairs[c]]

    def place(to_row, to_col):
        pltpu.make_async_remote_copy(
            src_ref=picked.at[to_col], dst_ref=spot,
            send_sem=place_sems.at[0], recv_sem=place_sems.at[1],
            device_id=(to_row, to_col), device_id_type=MESH,
        ).start()

    @pl.loop(1, COLS)
    def _(d):
        place(row, (col + d) % COLS)
        place(partner, (col + d) % COLS)

    place(partner, col)
    stay = pltpu.make_async_copy(picked.at[col], spot, own_sems.at[1])
    stay.start()
    pass_on(col, 1, right, 1)
    pass_on(col, 0, left, 2)
    stay.wait()
    arrived(landed.at[pl.ds(0, 2 * COLS - 1)], place_sems.at[1])

    x_side = (at(z, y, (x + 1) % NX), at(z, y, (x + NX - 1) % NX))
    z_side = (at((z + 1) % NZ, y, x), at((z + NZ - 1) % NZ, y, x))
    x_far = at(z, y, (x + 2) % NX)

    def x_from(way, hops):
        return (x + NX - hops) % NX if way == 0 else (x + hops) % NX

    def z_from(way, hops):
        return (z + NZ - hops) % NZ if way == 0 else (z + hops) % NZ

    def part_of(half):
        return pl.ds(0, RANK) if half is None else pl.ds(half * LANES, LANES)

    def small(panels, from_z, from_x, half=None):
        start = pl.multiple_of(from_z * SLAB + from_x * STEP, STEP)
        return theirs.at[:, panels, pl.ds(start, STEP), part_of(half)]

    def large(panel, from_z, half=None):
        start = pl.multiple_of(from_z * SLAB, SLAB)
        return theirs.at[:, panel, pl.ds(start, SLAB), part_of(half)]

    def shift(ref, sems, to_row):
        send(ref, ref, sems[0], sems[1], to_row, col)

    def narrow(first, size):
        panels = pl.ds(first, size)

        def begin():
            for v in WAYS:
                shift(small(panels, z, x), x_sems_of(v, 0), x_side[v])
            for v in WAYS:
                shift(small(panels, z, x, v), x_sems_of(v, 1), x_far)

        def turn():
            for v in WAYS:
                arrived(small(panels, z, x_from(v, 1)), x_sems_of(v, 0)[1])
                arrived(small(panels, z, x_from(v, 2), v), x_sems_of(v, 1)[1])
            for k in range(size):
                for v in WAYS:
                    shift(large(first + k, z), z_sems_of(v, k, 0), z_side[v])

        def relay(step, k, v):
            def run():
                arrived(large(first + k, z_from(v, step)), z_sems_of(v, k, step - 1)[1])
                half = v if step == 3 else None
                shift(large(first + k, z_from(v, step), half), z_sems_of(v, k, step), z_side[v])

            return run

        def end():
            for k in range(size):
                for v in WAYS:
                    arrived(large(first + k, z_from(v, 4), v), z_sems_of(v, k, 3)[1])

        relays = [relay(s, k, v) for s in (1, 2, 3) for k in range(size) for v in WAYS]
        return [begin, turn, *relays, end]

    def x_sems_of(v, slot):
        return x_sems.at[0, v, slot], x_sems.at[1, v, slot]

    def z_sems_of(v, k, slot):
        return z_sems.at[0, v, k, slot], z_sems.at[1, v, k, slot]

    def wide(group, first, size):
        panels = pl.ds(first, size)

        def along_z(v, slot):
            return wide_z_sems.at[group, 0, v, slot], wide_z_sems.at[group, 1, v, slot]

        def along_x(v, slot):
            return wide_x_sems.at[group, 0, v, slot], wide_x_sems.at[group, 1, v, slot]

        def sideways(slot):
            for v in WAYS:
                shift(small(panels, z_from(*ORDER[slot]), x), along_x(v, slot), x_side[v])

        def begin():
            for v in WAYS:
                shift(small(panels, z, x), along_z(v, 0), z_side[v])
            sideways(0)

        def relay(step, v):
            def run():
                arrived(small(panels, z_from(v, step), x), along_z(v, step - 1)[1])
                half = v if step == 3 else None
                shift(small(panels, z_from(v, step), x, half), along_z(v, step), z_side[v])
                sideways(ORDER.index((v, step)))

            return run

        def last():
            for v in WAYS:
                arrived(small(panels, z_from(v, 4), x, v), along_z(v, 3)[1])
            sideways(7)

        def hop(slot):
            def run():
                from_z, v = z_from(*ORDER[slot]), slot % 2
                for u in WAYS:
                    arrived(small(panels, from_z, x_from(u, 1)), along_x(u, slot)[1])
                shift(small(panels, from_z, x_from(v, 1)), along_x(v, 8 + slot // 2), x_side[v])

            return run

        def end():
            for slot in range(8):
                v = slot % 2
                block = small(panels, z_from(*ORDER[slot]), x_from(v, 2))
                arrived(block, along_x(v, 8 + slot // 2)[1])

        relays = [relay(s, v) for s in (1, 2, 3) for v in WAYS]
        return [begin, *relays, last], [*[hop(slot) for slot in range(8)], end]

    def onward(panel, part, slot, to, new_slot):
        def run():
            ring_arrived(panel, part, slot)
            pass_on(panel, part, to, new_slot)

        return run

    def cross_left():
        pass_on(col, 0, twin, 6)
        pass_on(col, 1, twin, 7)
        pass_on(left, 0, twin, 8)
        ring_arrived(left, 1, 1)
        pass_on(left, 1, twin, 9)

    def cross_right():
        pass_on(right, 1, twin, 11)
        ring_arrived(right, 0, 2)
        pass_on(right, 0, twin, 10)

    def ring_end():
        flip = 1 - 2 * core
        for panel, slot in ((twin, 6), (left + flip, 8), (right + flip, 10), (across + flip, 12)):
            ring_arrived(panel, 0, slot)
            ring_arrived(panel, 1, slot + 1)

    ring = [
        onward(left, 0, 0, right, 4), onward(right, 1, 3, left, 5), cross_left, cross_right,
        onward(across, 0, 4, twin, 12), onward(across, 1, 5, twin, 13), ring_end,
    ]
    flows = [narrow(*GROUPS[0]), *wide(0, *GROUPS[1]), *wide(1, *GROUPS[2]), ring]
    flows = [iter(flow) for flow in flows]

    def work(first, size):
        @pl.loop(first, first + size)
        def _(k):
            middle = lax.dot_general(
                mine[k, 0], theirs[0, k], (((0,), (0,)), ((), ())),
                preferred_element_type=jnp.float32,
            ).astype(jnp.bfloat16)
            mixed = jnp.dot(
                mine[k, 1], middle, preferred_element_type=jnp.float32
            ).astype(jnp.bfloat16)
            out[...] -= lax.dot_general(
                mixed, theirs[1, k], (((1,), (1,)), ((), ())), preferred_element_type=jnp.float32
            )

    for flow in PLAN[:-1]:
        next(flows[flow])()
    loads[3].wait()
    out[...] = base[...].astype(jnp.float32)
    work(0, GROUPS[2][0])
    next(flows[PLAN[-1]])()
    work(*GROUPS[2])

    for copy in sent:
        copy.wait_send()
    arrived(landed.at[pl.ds(0, ROWS - 1)], spread_sems.at[0])
    arrived(landed.at[pl.ds(0, 2 * COLS - 1)], place_sems.at[0])


def local(trailing, u_factor, w_factor, diag_inverse, ranks, col_rows):
    vmem, smem = pl.BlockSpec(memory_space=pltpu.VMEM), pl.BlockSpec(memory_space=pltpu.SMEM)
    anywhere = pl.BlockSpec(memory_space=pl.ANY)
    sems, half = pltpu.SemaphoreType.DMA, jnp.bfloat16
    return pl.pallas_call(
        kernel,
        out_shape=jax.ShapeDtypeStruct((TILE, TILE), jnp.float32),
        in_specs=[smem, smem, anywhere, anywhere, anywhere, anywhere],
        out_specs=vmem,
        scratch_shapes=[
            pltpu.VMEM((COLS, 2, TILE, RANK), half),
            pltpu.VMEM((2, COLS, TILE, RANK), half),
            pltpu.VMEM((ROWS, 2, STEP, LANES), half),
            pltpu.VMEM((COLS, 2, STEP, LANES), half),
            pltpu.VMEM((TILE, TILE), half),
            pltpu.VMEM((TILE, RANK), half),
            pltpu.VMEM((TILE, TILE), half),
            sems((4,)),
            sems((2,)),
            sems((2,)),
            sems((2,)),
            sems((2, 14)),
            sems((2, 2, 2)),
            sems((2, 2, GROUPS[0][1], 4)),
            sems((2, 2, 2, 12)),
            sems((2, 2, 2, 4)),
        ],
        compiler_params=pltpu.CompilerParams(
            collective_id=0, has_side_effects=True, vmem_limit_bytes=60 * 2**20
        ),
    )(col_rows, ranks, trailing, u_factor, w_factor, diag_inverse)


def solution(mesh):
    placed = (
        P("row", "col"),
        P("row", "col", None, None),
        P("row", "col", None, None),
        P("col", None, None),
        P("row", "col"),
        P(),
    )
    return jax.shard_map(
        local, mesh=mesh, in_specs=placed, out_specs=P("row", "col"), check_vma=False
    )
```

```python
import jax
import jax.numpy as jnp
from jax import lax
from jax.experimental import pallas as pl
from jax.experimental.pallas import tpu as pltpu
from jax.sharding import PartitionSpec as P

MESH = pl.DeviceIdType.MESH
ROWS, COLS = 64, 8
NX, NY, NZ, NH = 4, 2, 8, 4
TILE, RANK = 512, 256
LANES = RANK // NY
STEP = TILE // (NX * NZ)
SLAB = NX * STEP
WAYS = (0, 1)
GROUPS = ((0, 3), (3, 2), (5, 3))
PLAN = (
    0, 1, 3, 1, 1, 5, 5, 3, 3, 0, 2, 4, 1, 1, 2, 2, 3, 3, 4, 0, 0, 4, 0, 0, 0, 0, 2, 1, 1, 2, 3, 3,
    4, 0, 0, 4, 0, 0, 2, 0, 0, 2, 1, 3, 4, 0, 0, 4, 0, 5, 5, 0, 0, 0, 2, 4, 0, 2, 4,
)
ORDER = [(0, 0)] + [(w, s) for s in (1, 2, 3) for w in WAYS] + [(0, 4)]


def kernel(
    pairs, ranks, trailing, u_ref, w_ref, inverse_ref, out,
    mine, factors, turned, theirs, landed, picked, mixed, base, w, inverse,
    load_sems, own_sems, spread_sems, place_sems, ring_sems,
    x_sems, z_sems, wide_x_sems, wide_z_sems,
):
    row, col = lax.axis_index("row"), lax.axis_index("col")
    z, y, x = row // (NX * NY), (row // NX) % NY, row % NX
    h, core = col // 2, col % 2

    def at(new_z, new_y, new_x):
        return (new_z * NY + new_y) * NX + new_x

    partner = at(z, 1 - y, x)

    loads = [
        pltpu.make_async_copy(source, target, load_sems.at[i])
        for i, (source, target) in enumerate((
            (inverse_ref.at[0], inverse),
            (w_ref.at[0, 0], w),
            (u_ref.at[0, 0], mine.at[1]),
            (u_ref.at[0, 0], factors.at[col]),
            (trailing, base),
        ))
    ]
    for load in loads:
        load.start()

    barrier = pltpu.get_barrier_semaphore()

    @pl.loop(1, ROWS)
    def _(d):
        pl.semaphore_signal(barrier, inc=1, device_id=((row + d) % ROWS, col), device_id_type=MESH)

    @pl.loop(1, COLS)
    def _(d):
        other = (col + d) % COLS
        pl.semaphore_signal(barrier, inc=1, device_id=(row, other), device_id_type=MESH)
        pl.semaphore_signal(barrier, inc=1, device_id=(partner, other), device_id_type=MESH)

    loads[0].wait()
    loads[1].wait()
    product = jnp.dot(inverse[...], w[...], preferred_element_type=jnp.float32)
    lane = lax.broadcasted_iota(jnp.int32, (TILE, RANK), 1)
    solved = jnp.where(lane < ranks[0, 0], product, 0.0)
    mine[0] = solved.astype(jnp.bfloat16)
    turned[col] = solved.T.astype(jnp.bfloat16)
    loads[2].wait()
    loads[3].wait()

    pl.semaphore_wait(barrier, ROWS - 1 + 2 * (COLS - 1))

    sent = []

    def send(source, target, send_sem, recv_sem, to_row, to_col):
        copy = pltpu.make_async_remote_copy(
            src_ref=source, dst_ref=target, send_sem=send_sem, recv_sem=recv_sem,
            device_id=(to_row, to_col), device_id_type=MESH,
        )
        copy.start()
        sent.append(copy)

    def arrived(target, sem):
        pltpu.make_async_copy(target, target, sem).wait()

    def piece(other):
        place = (other // (NX * NY)) * NX + other % NX
        first = pl.multiple_of((other // NX) % NY * LANES, LANES)
        return mine.at[
            :, pl.ds(pl.multiple_of(place * STEP, STEP), STEP), pl.ds(first, LANES)
        ]

    own = pltpu.make_async_copy(piece(row), landed.at[row], own_sems.at[0])
    own.start()

    @pl.loop(1, ROWS)
    def _(d):
        other = (row + d) % ROWS
        pltpu.make_async_remote_copy(
            src_ref=piece(other), dst_ref=landed.at[row],
            send_sem=spread_sems.at[0], recv_sem=spread_sems.at[1],
            device_id=(other, col), device_id_type=MESH,
        ).start()

    right, left = ((h + 1) % NH) * 2 + core, ((h + NH - 1) % NH) * 2 + core
    across, twin = ((h + 2) % NH) * 2 + core, col + 1 - 2 * core
    count = [0]

    def row_factor(panel, part, quarter=None):
        ref = turned.at[panel] if part == 0 else factors.at[panel]
        if quarter is None:
            return ref
        height = ref.shape[0] // 4
        return ref.at[pl.ds(0, height)] if quarter == 0 else ref.at[pl.ds(height, 3 * height)]

    def pass_on(panel, part, to, slot, quarter=None):
        ref = row_factor(panel, part, quarter)
        send(ref, ref, ring_sems.at[0, count[0]], ring_sems.at[1, slot], row, to)
        count[0] += 1

    def ring_arrived(panel, part, slot, quarter=None):
        arrived(row_factor(panel, part, quarter), ring_sems.at[1, slot])

    pass_on(col, 0, right, 0)
    pass_on(col, 1, left, 3)

    own.wait()
    arrived(landed.at[pl.ds(0, ROWS - 1)], spread_sems.at[1])
    spot = theirs.at[
        :, col, pl.ds(pl.multiple_of((z * NX + x) * STEP, STEP), STEP),
        pl.ds(pl.multiple_of(y * LANES, LANES), LANES),
    ]
    for c in range(COLS):
        picked[c] = landed[pairs[c]]

    def place(to_row, to_col):
        pltpu.make_async_remote_copy(
            src_ref=picked.at[to_col], dst_ref=spot,
            send_sem=place_sems.at[0], recv_sem=place_sems.at[1],
            device_id=(to_row, to_col), device_id_type=MESH,
        ).start()

    @pl.loop(1, COLS)
    def _(d):
        place(row, (col + d) % COLS)
        place(partner, (col + d) % COLS)

    place(partner, col)
    stay = pltpu.make_async_copy(picked.at[col], spot, own_sems.at[1])
    stay.start()
    pass_on(col, 1, right, 14, 0)
    pass_on(col, 0, left, 15, 0)
    stay.wait()
    arrived(landed.at[pl.ds(0, 2 * COLS - 1)], place_sems.at[1])
    pass_on(col, 1, right, 1, 1)
    pass_on(col, 0, left, 2, 1)

    x_side = (at(z, y, (x + 1) % NX), at(z, y, (x + NX - 1) % NX))
    z_side = (at((z + 1) % NZ, y, x), at((z + NZ - 1) % NZ, y, x))
    x_far = at(z, y, (x + 2) % NX)

    def x_from(way, hops):
        return (x + NX - hops) % NX if way == 0 else (x + hops) % NX

    def z_from(way, hops):
        return (z + NZ - hops) % NZ if way == 0 else (z + hops) % NZ

    def part_of(half):
        return pl.ds(0, RANK) if half is None else pl.ds(half * LANES, LANES)

    def small(panels, from_z, from_x, half=None):
        start = pl.multiple_of(from_z * SLAB + from_x * STEP, STEP)
        return theirs.at[:, panels, pl.ds(start, STEP), part_of(half)]

    def large(panel, from_z, half=None):
        start = pl.multiple_of(from_z * SLAB, SLAB)
        return theirs.at[:, panel, pl.ds(start, SLAB), part_of(half)]

    def shift(ref, sems, to_row):
        send(ref, ref, sems[0], sems[1], to_row, col)

    def narrow(first, size):
        panels = pl.ds(first, size)

        def begin():
            for v in WAYS:
                shift(small(panels, z, x), x_sems_of(v, 0), x_side[v])
            for v in WAYS:
                shift(small(panels, z, x, v), x_sems_of(v, 1), x_far)

        def turn():
            for v in WAYS:
                arrived(small(panels, z, x_from(v, 1)), x_sems_of(v, 0)[1])
                arrived(small(panels, z, x_from(v, 2), v), x_sems_of(v, 1)[1])
            for k in range(size):
                for v in WAYS:
                    shift(large(first + k, z), z_sems_of(v, k, 0), z_side[v])

        def relay(step, k, v):
            def run():
                arrived(large(first + k, z_from(v, step)), z_sems_of(v, k, step - 1)[1])
                half = v if step == 3 else None
                shift(large(first + k, z_from(v, step), half), z_sems_of(v, k, step), z_side[v])

            return run

        def end():
            for k in range(size):
                for v in WAYS:
                    arrived(large(first + k, z_from(v, 4), v), z_sems_of(v, k, 3)[1])

        relays = [relay(s, k, v) for s in (1, 2, 3) for k in range(size) for v in WAYS]
        return [begin, turn, *relays, end]

    def x_sems_of(v, slot):
        return x_sems.at[0, v, slot], x_sems.at[1, v, slot]

    def z_sems_of(v, k, slot):
        return z_sems.at[0, v, k, slot], z_sems.at[1, v, k, slot]

    def wide(group, first, size):
        panels = pl.ds(first, size)

        def along_z(v, slot):
            return wide_z_sems.at[group, 0, v, slot], wide_z_sems.at[group, 1, v, slot]

        def along_x(v, slot):
            return wide_x_sems.at[group, 0, v, slot], wide_x_sems.at[group, 1, v, slot]

        def sideways(slot):
            for v in WAYS:
                shift(small(panels, z_from(*ORDER[slot]), x), along_x(v, slot), x_side[v])

        def begin():
            for v in WAYS:
                shift(small(panels, z, x), along_z(v, 0), z_side[v])
            sideways(0)

        def relay(step, v):
            def run():
                arrived(small(panels, z_from(v, step), x), along_z(v, step - 1)[1])
                half = v if step == 3 else None
                shift(small(panels, z_from(v, step), x, half), along_z(v, step), z_side[v])
                sideways(ORDER.index((v, step)))

            return run

        def last():
            for v in WAYS:
                arrived(small(panels, z_from(v, 4), x, v), along_z(v, 3)[1])
            sideways(7)

        def hop(slot):
            def run():
                from_z, v = z_from(*ORDER[slot]), slot % 2
                for u in WAYS:
                    arrived(small(panels, from_z, x_from(u, 1)), along_x(u, slot)[1])
                shift(small(panels, from_z, x_from(v, 1)), along_x(v, 8 + slot // 2), x_side[v])

            return run

        def end():
            for slot in range(8):
                v = slot % 2
                block = small(panels, z_from(*ORDER[slot]), x_from(v, 2))
                arrived(block, along_x(v, 8 + slot // 2)[1])

        relays = [relay(s, v) for s in (1, 2, 3) for v in WAYS]
        return [begin, *relays, last], [*[hop(slot) for slot in range(8)], end]

    def onward(panel, part, slot, to, new_slot):
        def run():
            ring_arrived(panel, part, slot)
            pass_on(panel, part, to, new_slot)

        return run

    def cross_left():
        pass_on(col, 0, twin, 6)
        pass_on(col, 1, twin, 7)
        pass_on(left, 0, twin, 8)
        ring_arrived(left, 1, 14, 0)
        ring_arrived(left, 1, 1, 1)
        pass_on(left, 1, twin, 9)

    def cross_right():
        pass_on(right, 1, twin, 11)
        ring_arrived(right, 0, 15, 0)
        ring_arrived(right, 0, 2, 1)
        pass_on(right, 0, twin, 10)

    def crossed(panel, slot):
        for part in (0, 1):
            ring_arrived(panel, part, slot + part)

    ring = [onward(left, 0, 0, right, 4), onward(right, 1, 3, left, 5), cross_left, cross_right]
    flows = [narrow(*GROUPS[0]), *wide(0, *GROUPS[1]), *wide(1, *GROUPS[2]), ring]
    flows = [iter(flow) for flow in flows]

    def work(*stops):
        panels = [2 * ((h + stop) % NH) + i for stop in stops for i in (0, 1)]
        for k in panels:
            middle = jnp.dot(turned[k], theirs[0, k], preferred_element_type=jnp.float32)
            middle = middle.astype(jnp.bfloat16)
            product = jnp.dot(factors[k], middle, preferred_element_type=jnp.float32)
            mixed[k] = product.astype(jnp.bfloat16)
        rows = jnp.concatenate([mixed[k] for k in panels], axis=1)
        cols = jnp.concatenate([theirs[1, k] for k in panels], axis=1)
        return lax.dot_general(
            rows, cols, (((1,), (1,)), ((), ())), preferred_element_type=jnp.float32
        )

    for flow in PLAN:
        next(flows[flow])()
    flip = 1 - 2 * core
    onward(across, 0, 4, twin, 12)()
    onward(across, 1, 5, twin, 13)()
    crossed(twin, 6)
    crossed(left + flip, 8)
    crossed(right + flip, 10)
    loads[4].wait()
    out[...] = base[...].astype(jnp.float32) - work(0, 1, 3)
    crossed(across + flip, 12)
    out[...] -= work(2)

    for copy in sent:
        copy.wait_send()
    arrived(landed.at[pl.ds(0, ROWS - 1)], spread_sems.at[0])
    arrived(landed.at[pl.ds(0, 2 * COLS - 1)], place_sems.at[0])


def local(trailing, u_factor, w_factor, diag_inverse, ranks, col_rows):
    vmem, smem = pl.BlockSpec(memory_space=pltpu.VMEM), pl.BlockSpec(memory_space=pltpu.SMEM)
    anywhere = pl.BlockSpec(memory_space=pl.ANY)
    sems, half = pltpu.SemaphoreType.DMA, jnp.bfloat16
    return pl.pallas_call(
        kernel,
        out_shape=jax.ShapeDtypeStruct((TILE, TILE), jnp.float32),
        in_specs=[smem, smem, anywhere, anywhere, anywhere, anywhere],
        out_specs=vmem,
        scratch_shapes=[
            pltpu.VMEM((2, TILE, RANK), half),
            pltpu.VMEM((COLS, TILE, RANK), half),
            pltpu.VMEM((COLS, RANK, TILE), half),
            pltpu.VMEM((2, COLS, TILE, RANK), half),
            pltpu.VMEM((ROWS, 2, STEP, LANES), half),
            pltpu.VMEM((COLS, 2, STEP, LANES), half),
            pltpu.VMEM((COLS, TILE, RANK), half),
            pltpu.VMEM((TILE, TILE), half),
            pltpu.VMEM((TILE, RANK), half),
            pltpu.VMEM((TILE, TILE), half),
            sems((5,)),
            sems((2,)),
            sems((2,)),
            sems((2,)),
            sems((2, 16)),
            sems((2, 2, 2)),
            sems((2, 2, GROUPS[0][1], 4)),
            sems((2, 2, 2, 12)),
            sems((2, 2, 2, 4)),
        ],
        compiler_params=pltpu.CompilerParams(
            collective_id=0, has_side_effects=True, vmem_limit_bytes=60 * 2**20
        ),
    )(col_rows, ranks, trailing, u_factor, w_factor, diag_inverse)


def solution(mesh):
    placed = (
        P("row", "col"),
        P("row", "col", None, None),
        P("row", "col", None, None),
        P("col", None, None),
        P("row", "col"),
        P(),
    )
    return jax.shard_map(
        local, mesh=mesh, in_specs=placed, out_specs=P("row", "col"), check_vma=False
    )
```

```python
import jax
import jax.numpy as jnp
from jax import lax
from jax.experimental import pallas as pl
from jax.experimental.pallas import tpu as pltpu
from jax.sharding import PartitionSpec as P

MESH = pl.DeviceIdType.MESH
ROWS, COLS = 64, 8
NX, NY, NZ, NH = 4, 2, 8, 4
TILE, RANK = 512, 256
LANES = RANK // NY
STEP = TILE // (NX * NZ)
SLAB = NX * STEP
WAYS = (0, 1)
GROUPS = ((0, 3), (3, 2), (5, 3))
PLAN = (
    0, 1, 3, 1, 1, 5, 5, 3, 3, 0, 2, 4, 1, 1, 2, 2, 3, 3, 4, 0, 0, 4, 0, 0, 0, 0, 2, 1, 1, 2, 3, 3,
    4, 0, 0, 4, 0, 0, 2, 0, 0, 2, 1, 3, 4, 0, 0, 4, 0, 5, 5, 0, 0, 0, 2, 4, 0, 2, 4,
)
ORDER = [(0, 0)] + [(w, s) for s in (1, 2, 3) for w in WAYS] + [(0, 4)]


def kernel(
    pairs, ranks, trailing, u_ref, w_ref, inverse_ref, out,
    mine, factors, turned, theirs, landed, picked, mixed, base, w, inverse,
    load_sems, own_sems, spread_sems, place_sems, ring_sems,
    x_sems, z_sems, wide_x_sems, wide_z_sems,
):
    row, col = lax.axis_index("row"), lax.axis_index("col")
    z, y, x = row // (NX * NY), (row // NX) % NY, row % NX
    h, core = col // 2, col % 2

    def at(new_z, new_y, new_x):
        return (new_z * NY + new_y) * NX + new_x

    partner = at(z, 1 - y, x)

    loads = [
        pltpu.make_async_copy(source, target, load_sems.at[i])
        for i, (source, target) in enumerate((
            (inverse_ref.at[0], inverse),
            (w_ref.at[0, 0], w),
            (u_ref.at[0, 0], mine.at[1]),
            (u_ref.at[0, 0], factors.at[col]),
            (trailing, base),
        ))
    ]
    for load in loads:
        load.start()

    barrier = pltpu.get_barrier_semaphore()

    @pl.loop(1, ROWS)
    def _(d):
        pl.semaphore_signal(barrier, inc=1, device_id=((row + d) % ROWS, col), device_id_type=MESH)

    @pl.loop(1, COLS)
    def _(d):
        other = (col + d) % COLS
        pl.semaphore_signal(barrier, inc=1, device_id=(row, other), device_id_type=MESH)
        pl.semaphore_signal(barrier, inc=1, device_id=(partner, other), device_id_type=MESH)

    loads[0].wait()
    loads[1].wait()
    product = jnp.dot(inverse[...], w[...], preferred_element_type=jnp.float32)
    lane = lax.broadcasted_iota(jnp.int32, (TILE, RANK), 1)
    solved = jnp.where(lane < ranks[0, 0], product, 0.0)
    mine[0] = solved.astype(jnp.bfloat16)
    turned[col] = solved.T.astype(jnp.bfloat16)
    loads[2].wait()
    loads[3].wait()

    pl.semaphore_wait(barrier, ROWS - 1 + 2 * (COLS - 1))

    sent = []

    def send(source, target, send_sem, recv_sem, to_row, to_col):
        copy = pltpu.make_async_remote_copy(
            src_ref=source, dst_ref=target, send_sem=send_sem, recv_sem=recv_sem,
            device_id=(to_row, to_col), device_id_type=MESH,
        )
        copy.start()
        sent.append(copy)

    def arrived(target, sem):
        pltpu.make_async_copy(target, target, sem).wait()

    def piece(other):
        place = (other // (NX * NY)) * NX + other % NX
        first = pl.multiple_of((other // NX) % NY * LANES, LANES)
        return mine.at[
            :, pl.ds(pl.multiple_of(place * STEP, STEP), STEP), pl.ds(first, LANES)
        ]

    own = pltpu.make_async_copy(piece(row), landed.at[row], own_sems.at[0])
    own.start()

    def spread(up, across_plane):
        other = at((z + up) % NZ, (y + across_plane // NX) % NY, (x + across_plane) % NX)
        pltpu.make_async_remote_copy(
            src_ref=piece(other), dst_ref=landed.at[row],
            send_sem=spread_sems.at[0], recv_sem=spread_sems.at[1],
            device_id=(other, col), device_id_type=MESH,
        ).start()

    for up in (4, 3, 5, 2, 6, 1, 7, 0):
        @pl.loop(1 if up == 0 else 0, NX * NY)
        def _(d):
            spread(up, d)

    right, left = ((h + 1) % NH) * 2 + core, ((h + NH - 1) % NH) * 2 + core
    across, twin = ((h + 2) % NH) * 2 + core, col + 1 - 2 * core
    count = [0]

    def row_factor(panel, part, quarter=None):
        ref = turned.at[panel] if part == 0 else factors.at[panel]
        if quarter is None:
            return ref
        height = ref.shape[0] // 4
        return ref.at[pl.ds(0, height)] if quarter == 0 else ref.at[pl.ds(height, 3 * height)]

    def pass_on(panel, part, to, slot, quarter=None):
        ref = row_factor(panel, part, quarter)
        send(ref, ref, ring_sems.at[0, count[0]], ring_sems.at[1, slot], row, to)
        count[0] += 1

    def ring_arrived(panel, part, slot, quarter=None):
        arrived(row_factor(panel, part, quarter), ring_sems.at[1, slot])

    pass_on(col, 0, right, 0)
    pass_on(col, 1, left, 3)

    own.wait()
    arrived(landed.at[pl.ds(0, ROWS - 1)], spread_sems.at[1])
    spot = theirs.at[
        :, col, pl.ds(pl.multiple_of((z * NX + x) * STEP, STEP), STEP),
        pl.ds(pl.multiple_of(y * LANES, LANES), LANES),
    ]
    for c in range(COLS):
        picked[c] = landed[pairs[c]]

    def place(to_row, to_col):
        pltpu.make_async_remote_copy(
            src_ref=picked.at[to_col], dst_ref=spot,
            send_sem=place_sems.at[0], recv_sem=place_sems.at[1],
            device_id=(to_row, to_col), device_id_type=MESH,
        ).start()

    for d in (4, 3, 5, 2, 6, 1, 7):
        place(row, (col + d) % COLS)
        place(partner, (col + d) % COLS)

    place(partner, col)
    stay = pltpu.make_async_copy(picked.at[col], spot, own_sems.at[1])
    stay.start()
    stay.wait()
    arrived(landed.at[pl.ds(0, 2 * COLS - 1)], place_sems.at[1])
    pass_on(col, 1, right, 14, 0)
    pass_on(col, 0, left, 15, 0)
    pass_on(col, 1, right, 1, 1)
    pass_on(col, 0, left, 2, 1)

    x_side = (at(z, y, (x + 1) % NX), at(z, y, (x + NX - 1) % NX))
    z_side = (at((z + 1) % NZ, y, x), at((z + NZ - 1) % NZ, y, x))
    x_far = at(z, y, (x + 2) % NX)

    def x_from(way, hops):
        return (x + NX - hops) % NX if way == 0 else (x + hops) % NX

    def z_from(way, hops):
        return (z + NZ - hops) % NZ if way == 0 else (z + hops) % NZ

    def part_of(half):
        return pl.ds(0, RANK) if half is None else pl.ds(half * LANES, LANES)

    def small(panels, from_z, from_x, half=None):
        start = pl.multiple_of(from_z * SLAB + from_x * STEP, STEP)
        return theirs.at[:, panels, pl.ds(start, STEP), part_of(half)]

    def large(panel, from_z, half=None):
        start = pl.multiple_of(from_z * SLAB, SLAB)
        return theirs.at[:, panel, pl.ds(start, SLAB), part_of(half)]

    def shift(ref, sems, to_row):
        send(ref, ref, sems[0], sems[1], to_row, col)

    def narrow(first, size):
        panels = pl.ds(first, size)

        def begin():
            for v in WAYS:
                shift(small(panels, z, x), x_sems_of(v, 0), x_side[v])
            for v in WAYS:
                shift(small(panels, z, x, v), x_sems_of(v, 1), x_far)

        def turn():
            for v in WAYS:
                arrived(small(panels, z, x_from(v, 1)), x_sems_of(v, 0)[1])
                arrived(small(panels, z, x_from(v, 2), v), x_sems_of(v, 1)[1])
            for k in range(size):
                for v in WAYS:
                    shift(large(first + k, z), z_sems_of(v, k, 0), z_side[v])

        def relay(step, k, v):
            def run():
                arrived(large(first + k, z_from(v, step)), z_sems_of(v, k, step - 1)[1])
                half = v if step == 3 else None
                shift(large(first + k, z_from(v, step), half), z_sems_of(v, k, step), z_side[v])

            return run

        def end():
            for k in range(size):
                for v in WAYS:
                    arrived(large(first + k, z_from(v, 4), v), z_sems_of(v, k, 3)[1])

        relays = [relay(s, k, v) for s in (1, 2, 3) for k in range(size) for v in WAYS]
        return [begin, turn, *relays, end]

    def x_sems_of(v, slot):
        return x_sems.at[0, v, slot], x_sems.at[1, v, slot]

    def z_sems_of(v, k, slot):
        return z_sems.at[0, v, k, slot], z_sems.at[1, v, k, slot]

    def wide(group, first, size):
        panels = pl.ds(first, size)

        def along_z(v, slot):
            return wide_z_sems.at[group, 0, v, slot], wide_z_sems.at[group, 1, v, slot]

        def along_x(v, slot):
            return wide_x_sems.at[group, 0, v, slot], wide_x_sems.at[group, 1, v, slot]

        def sideways(slot):
            for v in WAYS:
                shift(small(panels, z_from(*ORDER[slot]), x), along_x(v, slot), x_side[v])

        def begin():
            for v in WAYS:
                shift(small(panels, z, x), along_z(v, 0), z_side[v])
            sideways(0)

        def relay(step, v):
            def run():
                arrived(small(panels, z_from(v, step), x), along_z(v, step - 1)[1])
                half = v if step == 3 else None
                shift(small(panels, z_from(v, step), x, half), along_z(v, step), z_side[v])
                sideways(ORDER.index((v, step)))

            return run

        def last():
            for v in WAYS:
                arrived(small(panels, z_from(v, 4), x, v), along_z(v, 3)[1])
            sideways(7)

        def hop(slot):
            def run():
                from_z, v = z_from(*ORDER[slot]), slot % 2
                for u in WAYS:
                    arrived(small(panels, from_z, x_from(u, 1)), along_x(u, slot)[1])
                shift(small(panels, from_z, x_from(v, 1)), along_x(v, 8 + slot // 2), x_side[v])

            return run

        def end():
            for slot in range(8):
                v = slot % 2
                block = small(panels, z_from(*ORDER[slot]), x_from(v, 2))
                arrived(block, along_x(v, 8 + slot // 2)[1])

        relays = [relay(s, v) for s in (1, 2, 3) for v in WAYS]
        return [begin, *relays, last], [*[hop(slot) for slot in range(8)], end]

    def onward(panel, part, slot, to, new_slot):
        def run():
            ring_arrived(panel, part, slot)
            pass_on(panel, part, to, new_slot)

        return run

    def cross_left():
        pass_on(col, 0, twin, 6)
        pass_on(col, 1, twin, 7)
        pass_on(left, 0, twin, 8)
        ring_arrived(left, 1, 14, 0)
        ring_arrived(left, 1, 1, 1)
        pass_on(left, 1, twin, 9)

    def cross_right():
        pass_on(right, 1, twin, 11)
        ring_arrived(right, 0, 15, 0)
        ring_arrived(right, 0, 2, 1)
        pass_on(right, 0, twin, 10)

    def crossed(panel, slot):
        for part in (0, 1):
            ring_arrived(panel, part, slot + part)

    ring = [onward(left, 0, 0, right, 4), onward(right, 1, 3, left, 5), cross_left, cross_right]
    flows = [narrow(*GROUPS[0]), *wide(0, *GROUPS[1]), *wide(1, *GROUPS[2]), ring]
    flows = [iter(flow) for flow in flows]

    def work(*stops):
        panels = [2 * ((h + stop) % NH) + i for stop in stops for i in (0, 1)]
        for k in panels:
            middle = jnp.dot(turned[k], theirs[0, k], preferred_element_type=jnp.float32)
            middle = middle.astype(jnp.bfloat16)
            product = jnp.dot(factors[k], middle, preferred_element_type=jnp.float32)
            mixed[k] = product.astype(jnp.bfloat16)
        rows = jnp.concatenate([mixed[k] for k in panels], axis=1)
        cols = jnp.concatenate([theirs[1, k] for k in panels], axis=1)
        return lax.dot_general(
            rows, cols, (((1,), (1,)), ((), ())), preferred_element_type=jnp.float32
        )

    for flow in PLAN:
        next(flows[flow])()
    flip = 1 - 2 * core
    onward(across, 0, 4, twin, 12)()
    onward(across, 1, 5, twin, 13)()
    crossed(twin, 6)
    crossed(left + flip, 8)
    crossed(right + flip, 10)
    loads[4].wait()
    out[...] = base[...].astype(jnp.float32) - work(0, 1, 3)
    crossed(across + flip, 12)
    out[...] -= work(2)

    for copy in sent:
        copy.wait_send()
    arrived(landed.at[pl.ds(0, ROWS - 1)], spread_sems.at[0])
    arrived(landed.at[pl.ds(0, 2 * COLS - 1)], place_sems.at[0])


def local(trailing, u_factor, w_factor, diag_inverse, ranks, col_rows):
    vmem, smem = pl.BlockSpec(memory_space=pltpu.VMEM), pl.BlockSpec(memory_space=pltpu.SMEM)
    anywhere = pl.BlockSpec(memory_space=pl.ANY)
    sems, half = pltpu.SemaphoreType.DMA, jnp.bfloat16
    return pl.pallas_call(
        kernel,
        out_shape=jax.ShapeDtypeStruct((TILE, TILE), jnp.float32),
        in_specs=[smem, smem, anywhere, anywhere, anywhere, anywhere],
        out_specs=vmem,
        scratch_shapes=[
            pltpu.VMEM((2, TILE, RANK), half),
            pltpu.VMEM((COLS, TILE, RANK), half),
            pltpu.VMEM((COLS, RANK, TILE), half),
            pltpu.VMEM((2, COLS, TILE, RANK), half),
            pltpu.VMEM((ROWS, 2, STEP, LANES), half),
            pltpu.VMEM((COLS, 2, STEP, LANES), half),
            pltpu.VMEM((COLS, TILE, RANK), half),
            pltpu.VMEM((TILE, TILE), half),
            pltpu.VMEM((TILE, RANK), half),
            pltpu.VMEM((TILE, TILE), half),
            sems((5,)),
            sems((2,)),
            sems((2,)),
            sems((2,)),
            sems((2, 16)),
            sems((2, 2, 2)),
            sems((2, 2, GROUPS[0][1], 4)),
            sems((2, 2, 2, 12)),
            sems((2, 2, 2, 4)),
        ],
        compiler_params=pltpu.CompilerParams(
            collective_id=0, has_side_effects=True, vmem_limit_bytes=60 * 2**20
        ),
    )(col_rows, ranks, trailing, u_factor, w_factor, diag_inverse)


def solution(mesh):
    placed = (
        P("row", "col"),
        P("row", "col", None, None),
        P("row", "col", None, None),
        P("col", None, None),
        P("row", "col"),
        P(),
    )
    return jax.shard_map(
        local, mesh=mesh, in_specs=placed, out_specs=P("row", "col"), check_vma=False
    )
```

```python
import jax
import jax.numpy as jnp
from jax import lax
from jax.experimental import pallas as pl
from jax.experimental.pallas import tpu as pltpu
from jax.sharding import PartitionSpec as P

MESH = pl.DeviceIdType.MESH
ROWS, COLS = 64, 8
NX, NY, NZ, NH = 4, 2, 8, 4
TILE, RANK = 512, 256
LANES = RANK // NY
STEP = TILE // (NX * NZ)
SLAB = NX * STEP
WAYS = (0, 1)
GROUPS = ((0, 3), (3, 2), (5, 3))
PLAN = (
    0, 1, 3, 1, 1, 5, 5, 3, 3, 0, 2, 4, 1, 1, 2, 2, 3, 3, 4, 0, 0, 4, 0, 0, 0, 0, 2, 1, 1, 2, 3, 3,
    4, 0, 0, 4, 0, 0, 2, 0, 0, 2, 1, 3, 4, 0, 0, 4, 0, 5, 5, 0, 0, 0, 2, 4, 0, 2, 4,
)
ORDER = [(0, 0)] + [(w, s) for s in (1, 2, 3) for w in WAYS] + [(0, 4)]


def kernel(
    pairs, ranks, trailing, u_ref, w_ref, inverse_ref, out,
    mine, factors, turned, theirs, landed, picked, mixed, base, w, inverse,
    load_sems, own_sems, spread_sems, place_sems, ring_sems,
    x_sems, z_sems, wide_x_sems, wide_z_sems,
):
    row, col = lax.axis_index("row"), lax.axis_index("col")
    z, y, x = row // (NX * NY), (row // NX) % NY, row % NX
    h, core = col // 2, col % 2

    def at(new_z, new_y, new_x):
        return (new_z * NY + new_y) * NX + new_x

    partner = at(z, 1 - y, x)

    loads = [
        pltpu.make_async_copy(source, target, load_sems.at[i])
        for i, (source, target) in enumerate((
            (inverse_ref.at[0], inverse),
            (w_ref.at[0, 0], w),
            (u_ref.at[0, 0], mine.at[1]),
            (u_ref.at[0, 0], factors.at[col]),
            (trailing, base),
        ))
    ]
    for load in loads:
        load.start()

    barrier = pltpu.get_barrier_semaphore()

    @pl.loop(1, ROWS)
    def _(d):
        pl.semaphore_signal(barrier, inc=1, device_id=((row + d) % ROWS, col), device_id_type=MESH)

    @pl.loop(1, COLS)
    def _(d):
        other = (col + d) % COLS
        pl.semaphore_signal(barrier, inc=1, device_id=(row, other), device_id_type=MESH)
        pl.semaphore_signal(barrier, inc=1, device_id=(partner, other), device_id_type=MESH)

    loads[0].wait()
    loads[1].wait()
    product = jnp.dot(inverse[...], w[...], preferred_element_type=jnp.float32)
    lane = lax.broadcasted_iota(jnp.int32, (TILE, RANK), 1)
    solved = jnp.where(lane < ranks[0, 0], product, 0.0)
    mine[0] = solved.astype(jnp.bfloat16)
    turned[col] = solved.T.astype(jnp.bfloat16)
    loads[2].wait()
    loads[3].wait()

    pl.semaphore_wait(barrier, ROWS - 1 + 2 * (COLS - 1))

    sent = []

    def send(source, target, send_sem, recv_sem, to_row, to_col):
        copy = pltpu.make_async_remote_copy(
            src_ref=source, dst_ref=target, send_sem=send_sem, recv_sem=recv_sem,
            device_id=(to_row, to_col), device_id_type=MESH,
        )
        copy.start()
        sent.append(copy)

    def arrived(target, sem):
        pltpu.make_async_copy(target, target, sem).wait()

    def piece(other):
        place = (other // (NX * NY)) * NX + other % NX
        first = pl.multiple_of((other // NX) % NY * LANES, LANES)
        return mine.at[
            :, pl.ds(pl.multiple_of(place * STEP, STEP), STEP), pl.ds(first, LANES)
        ]

    own = pltpu.make_async_copy(piece(row), landed.at[row], own_sems.at[0])
    own.start()

    def spread(up, across_plane):
        other = at((z + up) % NZ, (y + across_plane // NX) % NY, (x + across_plane) % NX)
        pltpu.make_async_remote_copy(
            src_ref=piece(other), dst_ref=landed.at[row],
            send_sem=spread_sems.at[0], recv_sem=spread_sems.at[1],
            device_id=(other, col), device_id_type=MESH,
        ).start()

    for up in (4, 3, 5, 2, 6, 1, 7, 0):
        @pl.loop(1 if up == 0 else 0, NX * NY)
        def _(d):
            spread(up, d)

    right, left = ((h + 1) % NH) * 2 + core, ((h + NH - 1) % NH) * 2 + core
    across, twin = ((h + 2) % NH) * 2 + core, col + 1 - 2 * core
    count = [0]

    def row_factor(panel, part, quarter=None):
        ref = turned.at[panel] if part == 0 else factors.at[panel]
        if quarter is None:
            return ref
        height = ref.shape[0] // 4
        return ref.at[pl.ds(0, height)] if quarter == 0 else ref.at[pl.ds(height, 3 * height)]

    def pass_on(panel, part, to, slot, quarter=None):
        ref = row_factor(panel, part, quarter)
        send(ref, ref, ring_sems.at[0, count[0]], ring_sems.at[1, slot], row, to)
        count[0] += 1

    def ring_arrived(panel, part, slot, quarter=None):
        arrived(row_factor(panel, part, quarter), ring_sems.at[1, slot])

    pass_on(col, 0, right, 0)
    pass_on(col, 1, left, 3)

    own.wait()
    arrived(landed.at[pl.ds(0, ROWS - 1)], spread_sems.at[1])
    spot = theirs.at[
        :, col, pl.ds(pl.multiple_of((z * NX + x) * STEP, STEP), STEP),
        pl.ds(pl.multiple_of(y * LANES, LANES), LANES),
    ]
    for c in range(COLS):
        picked[c] = landed[pairs[c]]

    def place(to_row, to_col):
        pltpu.make_async_remote_copy(
            src_ref=picked.at[to_col], dst_ref=spot,
            send_sem=place_sems.at[0], recv_sem=place_sems.at[1],
            device_id=(to_row, to_col), device_id_type=MESH,
        ).start()

    for d in (4, 3, 5, 2, 6, 1, 7):
        place(row, (col + d) % COLS)
        place(partner, (col + d) % COLS)

    place(partner, col)
    stay = pltpu.make_async_copy(picked.at[col], spot, own_sems.at[1])
    stay.start()
    stay.wait()
    arrived(landed.at[pl.ds(0, 2 * COLS - 1)], place_sems.at[1])
    pass_on(col, 1, right, 14, 0)
    pass_on(col, 0, left, 15, 0)
    pass_on(col, 1, right, 1, 1)
    pass_on(col, 0, left, 2, 1)

    x_side = (at(z, y, (x + 1) % NX), at(z, y, (x + NX - 1) % NX))
    z_side = (at((z + 1) % NZ, y, x), at((z + NZ - 1) % NZ, y, x))
    x_far = at(z, y, (x + 2) % NX)

    def x_from(way, hops):
        return (x + NX - hops) % NX if way == 0 else (x + hops) % NX

    def z_from(way, hops):
        return (z + NZ - hops) % NZ if way == 0 else (z + hops) % NZ

    def part_of(half):
        return pl.ds(0, RANK) if half is None else pl.ds(half * LANES, LANES)

    def small(panels, from_z, from_x, half=None):
        start = pl.multiple_of(from_z * SLAB + from_x * STEP, STEP)
        return theirs.at[:, panels, pl.ds(start, STEP), part_of(half)]

    def large(panel, from_z, half=None):
        start = pl.multiple_of(from_z * SLAB, SLAB)
        return theirs.at[:, panel, pl.ds(start, SLAB), part_of(half)]

    def shift(ref, sems, to_row):
        send(ref, ref, sems[0], sems[1], to_row, col)

    def narrow(first, size):
        panels = pl.ds(first, size)

        def begin():
            for v in WAYS:
                shift(small(panels, z, x), x_sems_of(v, 0), x_side[v])
            for v in WAYS:
                shift(small(panels, z, x, v), x_sems_of(v, 1), x_far)

        def turn():
            for v in WAYS:
                arrived(small(panels, z, x_from(v, 1)), x_sems_of(v, 0)[1])
                arrived(small(panels, z, x_from(v, 2), v), x_sems_of(v, 1)[1])
            for k in range(size):
                for v in WAYS:
                    shift(large(first + k, z), z_sems_of(v, k, 0), z_side[v])

        def relay(step, k, v):
            def run():
                arrived(large(first + k, z_from(v, step)), z_sems_of(v, k, step - 1)[1])
                half = v if step == 3 else None
                shift(large(first + k, z_from(v, step), half), z_sems_of(v, k, step), z_side[v])

            return run

        def end():
            for k in range(size):
                for v in WAYS:
                    arrived(large(first + k, z_from(v, 4), v), z_sems_of(v, k, 3)[1])

        relays = [relay(s, k, v) for s in (1, 2, 3) for k in range(size) for v in WAYS]
        return [begin, turn, *relays, end]

    def x_sems_of(v, slot):
        return x_sems.at[0, v, slot], x_sems.at[1, v, slot]

    def z_sems_of(v, k, slot):
        return z_sems.at[0, v, k, slot], z_sems.at[1, v, k, slot]

    def wide(group, first, size):
        panels = pl.ds(first, size)

        def along_z(v, slot):
            return wide_z_sems.at[group, 0, v, slot], wide_z_sems.at[group, 1, v, slot]

        def along_x(v, slot):
            return wide_x_sems.at[group, 0, v, slot], wide_x_sems.at[group, 1, v, slot]

        def sideways(slot):
            for v in WAYS:
                shift(small(panels, z_from(*ORDER[slot]), x), along_x(v, slot), x_side[v])

        def begin():
            for v in WAYS:
                shift(small(panels, z, x), along_z(v, 0), z_side[v])
            sideways(0)

        def relay(step, v):
            def run():
                arrived(small(panels, z_from(v, step), x), along_z(v, step - 1)[1])
                half = v if step == 3 else None
                shift(small(panels, z_from(v, step), x, half), along_z(v, step), z_side[v])
                sideways(ORDER.index((v, step)))

            return run

        def last():
            for v in WAYS:
                arrived(small(panels, z_from(v, 4), x, v), along_z(v, 3)[1])
            sideways(7)

        def hop(slot):
            def run():
                from_z, v = z_from(*ORDER[slot]), slot % 2
                for u in WAYS:
                    arrived(small(panels, from_z, x_from(u, 1)), along_x(u, slot)[1])
                shift(small(panels, from_z, x_from(v, 1)), along_x(v, 8 + slot // 2), x_side[v])

            return run

        def end():
            for slot in range(8):
                v = slot % 2
                block = small(panels, z_from(*ORDER[slot]), x_from(v, 2))
                arrived(block, along_x(v, 8 + slot // 2)[1])

        relays = [relay(s, v) for s in (1, 2, 3) for v in WAYS]
        return [begin, *relays, last], [*[hop(slot) for slot in range(8)], end]

    def onward(panel, part, slot, to, new_slot):
        def run():
            ring_arrived(panel, part, slot)
            pass_on(panel, part, to, new_slot)

        return run

    def cross_left():
        pass_on(col, 0, twin, 6)
        pass_on(col, 1, twin, 7)
        pass_on(left, 0, twin, 8)
        ring_arrived(left, 1, 14, 0)
        ring_arrived(left, 1, 1, 1)
        pass_on(left, 1, twin, 9)

    def cross_right():
        pass_on(right, 1, twin, 11)
        ring_arrived(right, 0, 15, 0)
        ring_arrived(right, 0, 2, 1)
        pass_on(right, 0, twin, 10)

    def crossed(panel, slot):
        for part in (0, 1):
            ring_arrived(panel, part, slot + part)

    ring = [onward(left, 0, 0, right, 4), onward(right, 1, 3, left, 5), cross_left, cross_right]
    flows = [narrow(*GROUPS[0]), *wide(0, *GROUPS[1]), *wide(1, *GROUPS[2]), ring]
    flows = [iter(flow) for flow in flows]

    def work(*stops):
        panels = [2 * ((h + stop) % NH) + i for stop in stops for i in (0, 1)]
        for k in panels:
            middle = jnp.dot(turned[k], theirs[0, k], preferred_element_type=jnp.float32)
            middle = middle.astype(jnp.bfloat16)
            product = jnp.dot(factors[k], middle, preferred_element_type=jnp.float32)
            mixed[k] = product.astype(jnp.bfloat16)
        rows = jnp.concatenate([mixed[k] for k in panels], axis=1)
        cols = jnp.concatenate([theirs[1, k] for k in panels], axis=1)
        return lax.dot_general(
            rows, cols, (((1,), (1,)), ((), ())), preferred_element_type=jnp.float32
        )

    for flow in PLAN:
        next(flows[flow])()
    flip = 1 - 2 * core
    crossed(twin, 6)
    crossed(right + flip, 10)
    loads[4].wait()
    out[...] = base[...].astype(jnp.float32) - work(0, 1)
    onward(across, 0, 4, twin, 12)()
    onward(across, 1, 5, twin, 13)()
    crossed(left + flip, 8)
    out[...] -= work(3)
    crossed(across + flip, 12)
    out[...] -= work(2)

    for copy in sent:
        copy.wait_send()
    arrived(landed.at[pl.ds(0, ROWS - 1)], spread_sems.at[0])
    arrived(landed.at[pl.ds(0, 2 * COLS - 1)], place_sems.at[0])


def local(trailing, u_factor, w_factor, diag_inverse, ranks, col_rows):
    vmem, smem = pl.BlockSpec(memory_space=pltpu.VMEM), pl.BlockSpec(memory_space=pltpu.SMEM)
    anywhere = pl.BlockSpec(memory_space=pl.ANY)
    sems, half = pltpu.SemaphoreType.DMA, jnp.bfloat16
    return pl.pallas_call(
        kernel,
        out_shape=jax.ShapeDtypeStruct((TILE, TILE), jnp.float32),
        in_specs=[smem, smem, anywhere, anywhere, anywhere, anywhere],
        out_specs=vmem,
        scratch_shapes=[
            pltpu.VMEM((2, TILE, RANK), half),
            pltpu.VMEM((COLS, TILE, RANK), half),
            pltpu.VMEM((COLS, RANK, TILE), half),
            pltpu.VMEM((2, COLS, TILE, RANK), half),
            pltpu.VMEM((ROWS, 2, STEP, LANES), half),
            pltpu.VMEM((COLS, 2, STEP, LANES), half),
            pltpu.VMEM((COLS, TILE, RANK), half),
            pltpu.VMEM((TILE, TILE), half),
            pltpu.VMEM((TILE, RANK), half),
            pltpu.VMEM((TILE, TILE), half),
            sems((5,)),
            sems((2,)),
            sems((2,)),
            sems((2,)),
            sems((2, 16)),
            sems((2, 2, 2)),
            sems((2, 2, GROUPS[0][1], 4)),
            sems((2, 2, 2, 12)),
            sems((2, 2, 2, 4)),
        ],
        compiler_params=pltpu.CompilerParams(
            collective_id=0, has_side_effects=True, vmem_limit_bytes=60 * 2**20
        ),
    )(col_rows, ranks, trailing, u_factor, w_factor, diag_inverse)


def solution(mesh):
    placed = (
        P("row", "col"),
        P("row", "col", None, None),
        P("row", "col", None, None),
        P("col", None, None),
        P("row", "col"),
        P(),
    )
    return jax.shard_map(
        local, mesh=mesh, in_specs=placed, out_specs=P("row", "col"), check_vma=False
    )
```
